32 devices in a mesh: aa: 8 (over z, x), ba: 4 (over y, core).
Axes of the slice: x: 2, y: 2, z: 4, core: 2. Of those that a mesh axis runs over, the one named last changes fastest.
Arguments:
- features_a: bfloat16 [16, 32, 256], P('aa', 'ba'), may hold values from -9 to 9
- features_b: bfloat16 [16, 128, 256], P('ba', 'aa'), may hold values from -9 to 9
- conv_in: float32 [8, 3, 3, 3, 3], replicated, may hold values from -0.625 to 0.625
- bias_in: float32 [8], replicated, may hold values from -1 to 1
- conv_out: float32 [8, 3, 3, 3, 3], replicated, may hold values from -0.25 to 0.25
Outputs:
- log_mutual: float32 [16, 32, 16, 128], P('aa', None, 'ba')
- warped: float32 [16, 32, 256], P('aa', 'ba')
The draws below stay inside these ranges and needn't reach their ends.
All inputs are finite; a program needn't handle non-finite values.
Results may differ from the reference program's by a relative error of at most 0.0035.
Values may be sent and summed in bfloat16 or wider, within the bound.
No kernel may reach another device: no remote copies, remote signals or barrier semaphores. Data moves between devices by JAX's collectives and lax.ppermute only.
A program may use at most 64 MiB of HBM per device.

```python
import math
import jax
import jax.numpy as jnp
from jax import lax

C = 256
HID = 8
WA = 32
WB = 128
HA = 16
HB = 16


def draw_features_a(key, part):
    noise_key, scale_key = jax.random.split(jax.random.fold_in(key, 11))
    raw_noise = jax.random.truncated_normal(noise_key, -3.3, 3.3, (HA, WA, C))
    spread = jnp.exp(jax.random.uniform(scale_key, (HA, WA, 1), minval=math.log(0.4), maxval=math.log(2.0)))
    return (raw_noise * spread).astype(jnp.bfloat16)


def draw_features_b(key, part):
    noise_key, scale_key = jax.random.split(jax.random.fold_in(key, 13))
    raw_noise = jax.random.truncated_normal(noise_key, -3.3, 3.3, (HB, WB, C))
    spread = jnp.exp(jax.random.uniform(scale_key, (HB, WB, 1), minval=math.log(0.4), maxval=math.log(2.0)))
    return (raw_noise * spread).astype(jnp.bfloat16)


def scatter_about(key, shape, deviation, reach, held_as=jnp.bfloat16):
    values = deviation * jax.random.normal(key, shape, jnp.float32)
    return jnp.clip(values, min=-reach, max=reach).astype(held_as)


def setup_inputs(seed: int = 0) -> dict:
    seeds = jax.random.split(jax.random.key(seed), 6)
    features_a = draw_features_a(jax.random.fold_in(seeds[5], 71), 0)
    features_b = draw_features_b(jax.random.fold_in(seeds[5], 71), 0)
    conv_in = scatter_about(seeds[2], (HID, 3, 3, 3, 3), 81 ** -0.5, 0.625, jnp.float32)
    bias_in = jnp.clip(jax.random.uniform(seeds[3], (HID,), jnp.float32, -1.0, 1.0), -1.0, 1.0)
    conv_out = scatter_about(seeds[4], (HID, 3, 3, 3, 3), (HID * 81) ** -0.5, 0.25, jnp.float32)
    return dict(features_a=features_a, features_b=features_b, conv_in=conv_in, bias_in=bias_in, conv_out=conv_out)


def tap_offsets():
    return [(step_one, step_two, step_three, step_four) for step_one in range(3) for step_two in range(3) for step_three in range(3) for step_four in range(3)]

def window_sum(padded, kernel):
    extent = [size_here - 2 for size_here in padded.shape]
    result = jnp.zeros(extent, jnp.float32)
    for offsets in tap_offsets():
        window = padded[offsets[0]:offsets[0] + extent[0], offsets[1]:offsets[1] + extent[1], offsets[2]:offsets[2] + extent[2], offsets[3]:offsets[3] + extent[3]]
        result = result + kernel[offsets] * window
    return result

def dual_logsumexp(values):
    top_over_a = lax.optimization_barrier(jnp.max(values, axis=(0, 1), keepdims=True))
    norm_over_a = top_over_a + jnp.log(lax.optimization_barrier(jnp.sum(jnp.exp(values - top_over_a), axis=(0, 1), keepdims=True)))
    top_over_b = lax.optimization_barrier(jnp.max(values, axis=(2, 3), keepdims=True))
    norm_over_b = top_over_b + jnp.log(lax.optimization_barrier(jnp.sum(jnp.exp(values - top_over_b), axis=(2, 3), keepdims=True)))
    return (norm_over_a, norm_over_b)

def reference(features_a, features_b, conv_in, bias_in, conv_out):
    flat_a = features_a.reshape(HA * WA, C)
    flat_b = features_b.reshape(HB * WB, C)
    scores = (jnp.dot(flat_a, flat_b.T, preferred_element_type=jnp.float32) / math.sqrt(C)).reshape(HA, WA, HB, WB)
    offset = math.log(HA * WA * HB * WB)
    norm_a, norm_b = dual_logsumexp(scores)
    matched = jax.nn.softplus(2.0 * scores - norm_a - norm_b + offset)
    padded = jnp.pad(matched, 1)
    filtered = jnp.zeros(scores.shape, jnp.float32)
    for channel in range(HID):
        hidden = jax.nn.relu(window_sum(padded, conv_in[channel]) + bias_in[channel])
        filtered = filtered + window_sum(jnp.pad(hidden, 1), conv_out[channel])
    refined = scores + jax.nn.relu(filtered)
    norm_a2, norm_b2 = dual_logsumexp(refined)
    log_mutual = 2.0 * refined - norm_a2 - norm_b2 + offset
    weights = jnp.exp(refined - norm_b2).astype(jnp.bfloat16).reshape(HA * WA, HB * WB)
    warped = jnp.dot(weights, flat_b, preferred_element_type=jnp.float32).reshape(HA, WA, C)
    return (log_mutual, warped)
```

```python
import functools
import math

import jax
import jax.numpy as jnp
from jax import lax
from jax.experimental import pallas as pl
from jax.experimental.pallas import tpu as pltpu
from jax.sharding import PartitionSpec as P

F32 = jnp.float32
BF16 = jnp.bfloat16
NT = (((1,), (1,)), ((), ()))
NN = (((1,), (0,)), ((), ()))
BLOCK = 8
HALF = 64
LANES = 128


class Sizes:
    def __init__(self, rows_a, width_a, rows_b, width_b, channels, hidden, grid_a, grid_b):
        self.rows_a, self.width_a = rows_a, width_a
        self.rows_b, self.width_b = rows_b, width_b
        self.channels, self.hidden = channels, hidden
        self.grid_a, self.grid_b = grid_a, grid_b
        self.blocks = width_a // BLOCK
        self.halo_a = rows_a + 4
        self.halo_b = rows_b + 4
        self.mid_a = rows_a + 2
        self.mid_b = rows_b + 2
        self.span = BLOCK + 2
        self.lanes_in = self.blocks * HALF
        self.lanes_mid = hidden * self.mid_a * BLOCK
        self.cells_a = rows_a * width_a
        self.cells_b = rows_b * width_b
        self.offset = math.log(grid_a * width_a * grid_b * width_b)
        self.scale = 1.0 / math.sqrt(channels)
        assert self.halo_a * self.span <= HALF and self.cells_a == HALF
        assert width_b == LANES and self.lanes_mid % LANES == 0
        assert self.blocks % 2 == 0


def iota(shape, dim):
    return lax.broadcasted_iota(jnp.int32, shape, dim)


def over_span(index, span):
    return (index * (2048 // span + 1)) >> 11


def dot(left, right, dims=NN):
    return lax.dot_general(left, right, dims, preferred_element_type=F32)


def vmem_specs(count):
    return [pl.BlockSpec(memory_space=pltpu.VMEM)] * count


def smem_spec():
    return pl.BlockSpec(memory_space=pltpu.SMEM)


def patch_lanes(sz, shape, dim):
    index = iota(shape, dim)
    block = index >> 6
    inner = index & (HALF - 1)
    row = over_span(inner, sz.span)
    col = block * BLOCK + inner - row * sz.span - 1
    inside = (inner < sz.halo_a * sz.span) & (col >= 0) & (col < sz.width_a)
    return row, col, inside


def taps_kernel(sz, w_in_ref, w_out_ref, bias_ref, t_in_ref, t_out_ref, bias_row_ref, rows_ref, wide_ref):
    lanes = sz.lanes_mid
    per = sz.mid_a * BLOCK
    head = iota((sz.hidden, lanes), 0)
    lane = iota((sz.hidden, lanes), 1)
    pick = (lane >= head * per) & (lane < head * per + per)
    pick16 = pick.astype(F32).astype(BF16)
    rows_ref[...] = dot(w_in_ref[...].astype(BF16), pick16)
    bias_row_ref[...] = jnp.sum(jnp.where(pick, bias_ref[...], 0.0), axis=0, keepdims=True)
    inner = iota((HALF, lanes), 0)
    row_in = over_span(inner, sz.span)
    col_in = inner - row_in * sz.span
    lane = iota((HALF, lanes), 1)
    row_out = (lane // BLOCK) % sz.mid_a
    col_out = lane % BLOCK
    step_row = row_in - row_out
    step_col = col_in - col_out
    usable = inner < sz.halo_a * sz.span
    zeros = jnp.zeros((HALF, lanes), F32)
    for three in range(3):
        for four in range(3):
            total = zeros
            for one in range(3):
                for two in range(3):
                    tap = ((one * 3 + two) * 3 + three) * 3 + four
                    match = usable & (step_row == one) & (step_col == two)
                    total = jnp.where(match, rows_ref[tap : tap + 1, :], total)
            start = three * 4 * HALF + four * HALF
            t_in_ref[start : start + HALF, :] = total.astype(BF16)
        start = three * 4 * HALF + 3 * HALF
        t_in_ref[start : start + HALF, :] = zeros.astype(BF16)

    out_lanes = 4 * HALF
    unit = sz.rows_a * BLOCK
    group = 9 * sz.hidden
    for row in range(sz.mid_a):
        pair = iota((16, out_lanes), 0)
        lane = iota((16, out_lanes), 1)
        one = pair // 3
        four = pair - one * 3
        row_out = (lane % unit) // BLOCK
        hit = (pair < 9) & ((lane >> 6) == four) & (row - row_out == one)
        wide_ref[row * group : (row + 1) * group, :] = dot(
            w_out_ref[...].astype(BF16), hit.astype(F32).astype(BF16)
        )
    lane = iota((BLOCK, out_lanes), 1)
    col_out = ((lane & (HALF - 1)) // unit) * BLOCK + lane % BLOCK
    for block in range(sz.blocks):
        step = iota((BLOCK, out_lanes), 0) + block * BLOCK - col_out + 1
        for three in range(3):
            for head in range(sz.hidden):
                for row in range(0, sz.mid_a, 2):
                    parts = []
                    for sub in (row, row + 1):
                        total = jnp.zeros((BLOCK, out_lanes), F32)
                        for two in range(3):
                            at = sub * group + (two * 3 + three) * sz.hidden + head
                            total = jnp.where(step == two, wide_ref[at : at + 1, :], total)
                        parts.append(total)
                    start = three * sz.blocks * lanes + block * lanes + head * per + row * BLOCK
                    t_out_ref[start : start + 2 * BLOCK, :] = jnp.concatenate(parts, 0).astype(BF16)


def build_taps(sz, conv_in, bias_in, conv_out):
    hidden = conv_in.shape[0]
    w_in = jnp.transpose(conv_in, (1, 2, 3, 4, 0)).reshape(81, hidden)
    w_out = jnp.transpose(conv_out, (2, 3, 0, 1, 4)).reshape(9 * hidden, 9)
    w_out = jnp.pad(w_out, ((0, 0), (0, 7)))
    rows_in = 3 * 4 * HALF
    rows_out = 3 * sz.blocks * sz.lanes_mid
    return pl.pallas_call(
        functools.partial(taps_kernel, sz),
        out_shape=(
            jax.ShapeDtypeStruct((rows_in, sz.lanes_mid), BF16),
            jax.ShapeDtypeStruct((rows_out, 4 * HALF), BF16),
            jax.ShapeDtypeStruct((1, sz.lanes_mid), F32),
        ),
        in_specs=vmem_specs(3),
        out_specs=tuple(vmem_specs(3)),
        scratch_shapes=[
            pltpu.VMEM((81, sz.lanes_mid), F32),
            pltpu.VMEM((sz.mid_a * 9 * hidden, 4 * HALF), F32),
        ],
        name="taps",
    )(w_in, w_out, bias_in.reshape(hidden, 1))


def scores_body(sz, rank_ref, norm_rows, patch_rows, tile_b, u_ref, part_ref, own_ref):
    channels = sz.channels
    source = patch_rows.shape[0]
    row, col, inside = patch_lanes(sz, (sz.lanes_in, source), 0)
    at = iota((sz.lanes_in, source), 1)
    wanted = (col >> 3) * (sz.halo_a * BLOCK) + row * BLOCK + (col & (BLOCK - 1))
    pick = (inside & (at == wanted)).astype(F32).astype(BF16)
    patches = dot(pick, patch_rows[...]).astype(BF16)
    chunk = 512
    chunks = norm_rows.shape[0] // chunk

    def per_row(index, carry):
        rows = tile_b[pl.ds(pl.multiple_of(index * LANES, LANES), LANES), :]

        def per_chunk(step, state):
            best, mass = state
            block = norm_rows[pl.ds(pl.multiple_of(step * chunk, chunk), chunk), :]
            scores = dot(rows, block, NT) * sz.scale
            fresh = jnp.maximum(best, jnp.max(scores, axis=1, keepdims=True))
            mass = mass * jnp.exp(best - fresh) + jnp.sum(jnp.exp(scores - fresh), axis=1, keepdims=True)
            return fresh, mass

        if chunks == 1:
            scores = dot(rows, norm_rows[...], NT) * sz.scale
            best = jnp.max(scores, axis=1, keepdims=True)
            mass = jnp.sum(jnp.exp(scores - best), axis=1, keepdims=True)
        else:
            start = jnp.full((LANES, 1), -jnp.inf, F32), jnp.zeros((LANES, 1), F32)
            best, mass = lax.fori_loop(0, chunks, per_chunk, start)
        norm_a = best + jnp.log(mass)
        near = dot(rows, patches, NT) * sz.scale
        place = pl.ds(pl.multiple_of(index * LANES, LANES), LANES)
        own_ref[place, :] = near
        u_ref[place, :] = 2.0 * near - norm_a + sz.offset
        return carry

    lax.fori_loop(0, sz.halo_b, per_row, 0)
    own = own_ref[2 * LANES : (2 + sz.rows_b) * LANES, :]
    best = jnp.max(own, axis=0, keepdims=True)
    mass = jnp.sum(jnp.exp(own - best), axis=0, keepdims=True)
    part_ref[...] = jnp.concatenate(
        [best, mass, jnp.zeros((6, sz.lanes_in), F32)], axis=0
    )


def scores_kernel_direct(sz, rank_ref, norm_rows, patch_rows, tile_b, u_ref, part_ref, own_ref):
    scores_body(sz, rank_ref, norm_rows, patch_rows, tile_b, u_ref, part_ref, own_ref)


def scores_kernel_pieces(
    sz, count, rank_ref, own_piece, core_piece, cross_piece, diag_piece,
    u_ref, part_ref, own_a_ref, own_b_ref,
    norm_rows, patch_rows, tile_b, near_ref,
):
    row_rank, col_rank = rank_ref[0], rank_ref[1]
    cells = sz.rows_a * BLOCK
    cols = sz.width_b // count
    pieces = ((own_piece, 0), (core_piece, 1), (diag_piece, 2), (cross_piece, 3))
    for order, (piece, flip) in enumerate(pieces):
        norm_rows[order * count * cells : (order + 1) * count * cells, :] = piece[
            :, 0:cells, :
        ].reshape(count * cells, sz.channels)
        block = col_rank ^ flip
        for step in range(3):
            where_from = jnp.clip(row_rank - 1 + step, 0, count - 1)
            start = pl.multiple_of(block * (3 * cells) + step * cells, cells)
            patch_rows[pl.ds(start, cells), :] = piece[where_from, 0:cells, :]
        start = pl.multiple_of(block * cells, cells)
        own_a_ref[pl.ds(start, cells), :] = piece[row_rank, 0:cells, :]
    width = sz.width_b
    for row in range(sz.rows_b):
        rows = own_piece[:, cells + row * cols : cells + (row + 1) * cols, :].reshape(width, sz.channels)
        tile_b[(2 + row) * width : (3 + row) * width, :] = rows
        own_b_ref[row * width : (row + 1) * width, :] = rows
    odd = col_rank & 1
    far = (2 + sz.rows_b) * width
    for piece, base in ((core_piece, (1 - odd) * far), (cross_piece, odd * far)):
        for row in range(2):
            rows = piece[:, cells + row * cols : cells + (row + 1) * cols, :].reshape(width, sz.channels)
            tile_b[pl.ds(pl.multiple_of(base + row * width, width), width), :] = rows
    scores_body(sz, rank_ref, norm_rows, patch_rows, tile_b, u_ref, part_ref, near_ref)


def softplus(values):
    return jnp.maximum(values, 0.0) + jnp.log1p(jnp.exp(-jnp.abs(values)))


def refine_kernel(sz, parts, split, rank_ref, u_ref, *refs):
    part_refs = refs[:parts]
    t_in, t_out, bias_row, own_a, own_b = refs[parts : parts + 5]
    outs = refs[parts + 5 : -4]
    refined_ref, sums_a_ref = outs[0], outs[1]
    x_ref, mid_ref, share_ref, stat_ref = refs[-4:]
    row_rank, col_rank = rank_ref[0], rank_ref[1]
    last = sz.grid_b // sz.rows_b - 1
    tops, masses = [], []
    for ref in part_refs:
        for at in range(ref.shape[0] // 8):
            tops.append(ref[at * 8 : at * 8 + 1, :])
            masses.append(ref[at * 8 + 1 : at * 8 + 2, :])
    top = functools.reduce(jnp.maximum, tops)
    mass = sum(m * jnp.exp(t - top) for t, m in zip(tops, masses))
    norm_b = top + jnp.log(mass)

    row, _, inside = patch_lanes(sz, (1, sz.lanes_in), 1)
    row = row + row_rank * sz.rows_a - 2
    inside = inside & (row >= 0) & (row < sz.grid_a)
    lane = iota((LANES, LANES), 1)
    line = iota((LANES, LANES), 0)
    low = lane < HALF
    low_down = low & (line > 0)
    low_up = low & (line < LANES - 1)

    def place_matched(index, carry):
        place = pl.ds(pl.multiple_of(index * LANES, LANES), LANES)
        matched = softplus(u_ref[place, :] - norm_b)
        matched = jnp.where(inside, matched, 0.0)
        for pair in range(sz.blocks // 2):
            here = matched[:, pair * LANES : (pair + 1) * LANES]
            turned = pltpu.roll(here, HALF, 1)
            for side, (one, two) in enumerate(((here, turned), (turned, here))):
                block = pair * 2 + side
                first = jnp.where(low, jnp.where(low_down, pltpu.roll(one, 1, 0), 0.0), two)
                second = jnp.where(low_up, pltpu.roll(one, LANES - 1, 0), 0.0)
                x_ref[block, place, 0:LANES] = first.astype(BF16)
                x_ref[block, place, LANES : 2 * LANES] = second.astype(BF16)
        return carry

    lax.fori_loop(0, sz.halo_b, place_matched, 0)
    edge = 2 * LANES
    far = (2 + sz.rows_b) * LANES

    @pl.when(col_rank == 0)
    def _():
        x_ref[:, 0:edge, :] = jnp.zeros((sz.blocks, edge, 2 * LANES), BF16)

    @pl.when(col_rank == last)
    def _():
        x_ref[:, far : far + edge, :] = jnp.zeros((sz.blocks, edge, 2 * LANES), BF16)

    rows_mid = sz.mid_b * LANES
    lane = iota((1, sz.lanes_mid), 1)
    row = (lane // BLOCK) % sz.mid_a + row_rank * sz.rows_a - 1
    inside_mid = (row >= 0) & (row < sz.grid_a)
    bias = bias_row[...]
    for block in range(sz.blocks):
        total = bias
        for three in range(3):
            total = total + dot(
                x_ref[block, three * LANES : three * LANES + rows_mid, :],
                t_in[three * 4 * HALF : (three + 1) * 4 * HALF, :],
            )
        hidden = jnp.where(inside_mid, jnp.maximum(total, 0.0), 0.0)
        mid_ref[:, block * sz.lanes_mid : (block + 1) * sz.lanes_mid] = hidden.astype(BF16)
    wide = sz.blocks * sz.lanes_mid

    @pl.when(col_rank == 0)
    def _():
        mid_ref[0:LANES, :] = jnp.zeros((LANES, wide), BF16)

    @pl.when(col_rank == last)
    def _():
        mid_ref[rows_mid - LANES : rows_mid, :] = jnp.zeros((LANES, wide), BF16)

    spread = 0.0
    for three in range(3):
        spread = spread + dot(
            mid_ref[three * LANES : three * LANES + sz.cells_b, :],
            t_out[three * wide : (three + 1) * wide, :],
        )
    best_b = None
    for row in range(sz.rows_b):
        left = spread[row * LANES : (row + 1) * LANES, 0:LANES]
        right = spread[row * LANES : (row + 1) * LANES, LANES : 2 * LANES]
        filtered = (
            jnp.where(line > 0, pltpu.roll(left, 1, 0), 0.0)
            + pltpu.roll(left, HALF, 1)
            + jnp.where(line < LANES - 1, pltpu.roll(right, LANES - 1, 0), 0.0)
        )
        filtered = jnp.maximum(filtered, 0.0).T[0:HALF, :]
        scores = dot(own_a[...], own_b[row * LANES : (row + 1) * LANES, :], NT) * sz.scale
        refined = scores + filtered
        refined_ref[:, row * LANES : (row + 1) * LANES] = refined
        top = jnp.max(refined, axis=0, keepdims=True)
        sums_a_ref[row : row + 1, :] = top
        sums_a_ref[sz.rows_b + row : sz.rows_b + row + 1, :] = jnp.sum(
            jnp.exp(refined - top), axis=0, keepdims=True
        )
        best = jnp.max(refined, axis=1, keepdims=True)
        best_b = best if best_b is None else jnp.maximum(best_b, best)
    weights = jnp.exp(refined_ref[...] - best_b)
    total_b = jnp.sum(weights, axis=1, keepdims=True)
    high = weights.astype(BF16)
    rest = (weights - high.astype(F32)).astype(BF16)
    share = dot(high, own_b[...]) + dot(rest, own_b[...])
    lane = iota((HALF, LANES), 1)
    stats = jnp.where(lane < HALF, best_b, total_b)
    if not split:
        outs[2][...] = share
        outs[3][...] = stats
        return
    share_ref[...] = share
    cells = sz.rows_a * BLOCK
    for flip in range(4):
        out = outs[2 + flip]
        start = pl.multiple_of((col_rank ^ flip) * cells, cells)
        out[0:cells, :] = share_ref[pl.ds(start, cells), :]
        out[cells:, 0:LANES] = stats[0 : HALF // 2, :]
        out[cells:, LANES:] = stats[HALF // 2 :, :]


def finish_kernel(sz, count, rank_ref, refined_ref, sums_ref, own, core, diag, cross, out_ref, warped_ref, stat_ref):
    col_rank = rank_ref[1]
    cells = sz.rows_a * BLOCK
    lane = iota((HALF, LANES), 1)
    tops, masses = [], []
    for at, ref in enumerate((own, core, diag, cross)):
        stats = jnp.concatenate([ref[cells:, 0:LANES], ref[cells:, LANES:]], axis=0)
        turned = pltpu.roll(stats, HALF, 1)
        tops.append(jnp.where(lane < HALF, stats, turned))
        masses.append(jnp.where(lane < HALF, turned, stats))
        stat_ref[at] = tops[-1]
    top = functools.reduce(jnp.maximum, tops)
    norm_b = top + jnp.log(sum(m * jnp.exp(t - top) for t, m in zip(tops, masses)))
    stat_ref[4] = norm_b
    mine = pl.ds(pl.multiple_of(col_rank * cells, cells), cells)
    norm_mine = stat_ref[4, mine, :]
    warped = 0.0
    for at, ref in enumerate((own, core, diag, cross)):
        factor = jnp.exp(stat_ref[at, mine, :] - norm_mine)
        warped = warped + ref[0:cells, :] * jnp.concatenate(
            [factor] * (sz.channels // LANES), axis=1
        )
    warped_ref[...] = warped.reshape(sz.rows_a, BLOCK, sz.channels)
    tops = [sums_ref[at * 8 : at * 8 + sz.rows_b, :] for at in range(count)]
    masses = [sums_ref[at * 8 + sz.rows_b : at * 8 + 2 * sz.rows_b, :] for at in range(count)]
    top = functools.reduce(jnp.maximum, tops)
    norm_a = top + jnp.log(sum(m * jnp.exp(t - top) for t, m in zip(tops, masses)))
    for row in range(sz.rows_b):
        values = (
            2.0 * refined_ref[:, row * LANES : (row + 1) * LANES]
            - norm_a[row : row + 1, :]
            - norm_b
            + sz.offset
        )
        for block in range(sz.blocks):
            for high in range(sz.rows_a):
                start = block * cells + high * BLOCK
                out_ref[high, block * BLOCK : (block + 1) * BLOCK, row, :] = values[start : start + BLOCK, :]


def call(kernel, name, outs, scratch, *args):
    return pl.pallas_call(
        kernel,
        out_shape=outs,
        in_specs=[smem_spec()] + vmem_specs(len(args) - 1),
        out_specs=tuple(vmem_specs(len(outs))),
        scratch_shapes=scratch,
        name=name,
    )(*args)


def refine_call(sz, parts, split, *args):
    shape = jax.ShapeDtypeStruct
    cells = sz.rows_a * BLOCK
    outs = [shape((HALF, sz.cells_b), F32), shape((8, LANES), F32)]
    if split:
        outs += [shape((cells + HALF // 2, 2 * LANES), F32)] * 4
    else:
        outs += [shape((HALF, sz.channels), F32), shape((HALF, LANES), F32)]
    scratch = [
        pltpu.VMEM((sz.blocks, sz.halo_b * LANES, 2 * LANES), BF16),
        pltpu.VMEM((sz.mid_b * LANES, sz.blocks * sz.lanes_mid), BF16),
        pltpu.VMEM((HALF, sz.channels), F32),
        pltpu.VMEM((HALF, LANES), F32),
    ]
    return call(functools.partial(refine_kernel, sz, parts, split), "refine", tuple(outs), scratch, *args)


def swap(value, flip, count):
    return lax.ppermute(value, "ba", [(at, at ^ flip) for at in range(count)])


def sizes_of(features_a, features_b, conv_in):
    rows_a, cols_a, channels = features_a.shape
    rows_b, cols_b, _ = features_b.shape
    count_a, count_b = lax.axis_size("aa"), lax.axis_size("ba")
    return Sizes(
        rows_a, cols_a * count_b, rows_b, cols_b * count_a, channels, conv_in.shape[0],
        rows_a * count_a, rows_b * count_b,
    )


def local_four(features_a, features_b, conv_in, bias_in, conv_out):
    sz = sizes_of(features_a, features_b, conv_in)
    count = lax.axis_size("aa")
    shape = jax.ShapeDtypeStruct
    row_rank, col_rank = lax.axis_index("aa"), lax.axis_index("ba")
    rank = jnp.stack([row_rank, col_rank]).astype(jnp.int32)
    cells = sz.rows_a * BLOCK
    cols = features_b.shape[1]
    mine = jnp.concatenate(
        [features_a.reshape(cells, sz.channels), features_b.reshape(-1, sz.channels)], axis=0
    )
    spread = jnp.broadcast_to(mine[None], (count,) + mine.shape)
    own = lax.all_to_all(spread, "aa", 0, 0, tiled=True)
    rows_here = own[:, 0:cells]
    first = own[:, cells : cells + 2 * cols]
    final = own[:, cells + (sz.rows_b - 2) * cols :]
    odd = (col_rank & 1) == 1
    core = swap(jnp.concatenate([rows_here, jnp.where(odd, first, final)], axis=1), 1, 4)
    cross = swap(jnp.concatenate([rows_here, jnp.where(odd, final, first)], axis=1), 3, 4)
    diag = swap(rows_here, 2, 4)
    t_in, t_out, bias_row = build_taps(sz, conv_in, bias_in, conv_out)
    u, part, own_a, own_b = call(
        functools.partial(scores_kernel_pieces, sz, count),
        "scores",
        (
            shape((sz.halo_b * LANES, sz.lanes_in), F32),
            shape((8, sz.lanes_in), F32),
            shape((HALF, sz.channels), BF16),
            shape((sz.cells_b, sz.channels), BF16),
        ),
        [
            pltpu.VMEM((sz.grid_a * sz.width_a, sz.channels), BF16),
            pltpu.VMEM((sz.halo_a * sz.width_a, sz.channels), BF16),
            pltpu.VMEM((sz.halo_b * LANES, sz.channels), BF16),
            pltpu.VMEM((sz.halo_b * LANES, sz.lanes_in), F32),
        ],
        rank, own, core, cross, diag,
    )
    others = [swap(part, flip, 4) for flip in (1, 3, 2)]
    refined, sums_a, *bundles = refine_call(
        sz, 4, True, rank, u, part, *others, t_in, t_out, bias_row, own_a, own_b
    )
    moved = [swap(bundles[flip], flip, 4) for flip in (1, 3, 2)]
    sums = jnp.broadcast_to(sums_a[None], (count,) + sums_a.shape)
    sums = lax.all_to_all(sums, "aa", 0, 0, tiled=True).reshape(count * 8, LANES)
    return call(
        functools.partial(finish_kernel, sz, count),
        "finish",
        (
            shape((sz.rows_a, sz.width_a, sz.rows_b, LANES), F32),
            shape((sz.rows_a, BLOCK, sz.channels), F32),
        ),
        [pltpu.VMEM((5, HALF, LANES), F32)],
        rank, refined, sums, bundles[0], moved[0], moved[2], moved[1],
    )


def local_any(features_a, features_b, conv_in, bias_in, conv_out):
    sz = sizes_of(features_a, features_b, conv_in)
    count_b = lax.axis_size("ba")
    shape = jax.ShapeDtypeStruct
    row_rank, col_rank = lax.axis_index("aa"), lax.axis_index("ba")
    rank = jnp.stack([row_rank, col_rank]).astype(jnp.int32)
    channels = sz.channels
    rows_a = lax.all_gather(features_a, "ba", axis=1, tiled=True)
    all_a = lax.all_gather(rows_a, "aa", axis=0, tiled=True)
    around = lax.dynamic_slice_in_dim(
        jnp.pad(all_a, ((2, 2), (0, 0), (0, 0))), row_rank * sz.rows_a, sz.halo_a, axis=0
    )

    def blocked(rows):
        split = rows.reshape(rows.shape[0], sz.blocks, BLOCK, channels)
        return jnp.transpose(split, (1, 0, 2, 3)).reshape(-1, channels)

    rows_b = lax.all_gather(features_b, "aa", axis=1, tiled=True)
    ends = count_b - 1
    before = lax.ppermute(rows_b[-2:], "ba", [(at, at + 1) for at in range(ends)])
    after = lax.ppermute(rows_b[:2], "ba", [(at + 1, at) for at in range(ends)])
    tile_b = jnp.concatenate([before, rows_b, after], axis=0).reshape(-1, channels)
    t_in, t_out, bias_row = build_taps(sz, conv_in, bias_in, conv_out)
    u, part = call(
        functools.partial(scores_kernel_direct, sz),
        "scores",
        (shape((sz.halo_b * LANES, sz.lanes_in), F32), shape((8, sz.lanes_in), F32)),
        [pltpu.VMEM((sz.halo_b * LANES, sz.lanes_in), F32)],
        rank, all_a.reshape(-1, channels), blocked(around), tile_b,
    )
    parts = lax.all_gather(part, "ba", axis=0, tiled=True)
    refined, sums_a, share, stats = refine_call(
        sz, 1, False, rank, u, parts, t_in, t_out, bias_row, blocked(rows_a), rows_b.reshape(-1, channels)
    )
    top, mass = stats[:, 0], stats[:, HALF]
    best = lax.pmax(top, "ba")
    norm_b = best + jnp.log(lax.psum(mass * jnp.exp(top - best), "ba"))

    def unblocked(rows):
        split = rows.reshape((sz.blocks, sz.rows_a, BLOCK) + rows.shape[1:])
        return jnp.swapaxes(split, 0, 1).reshape((sz.rows_a, sz.width_a) + rows.shape[1:])

    share = unblocked(share * jnp.exp(top - norm_b)[:, None])
    warped = lax.psum_scatter(share, "ba", scatter_dimension=1, tiled=True)
    top, mass = sums_a[: sz.rows_b], sums_a[sz.rows_b : 2 * sz.rows_b]
    best = lax.pmax(top, "aa")
    norm_a = best + jnp.log(lax.psum(mass * jnp.exp(top - best), "aa"))
    refined = refined.reshape(HALF, sz.rows_b, LANES)
    mutual = 2.0 * refined - norm_a - norm_b[:, None, None] + sz.offset
    return unblocked(mutual), warped


def local(features_a, features_b, *rest):
    suits = lax.axis_size("ba") == 4 and features_a.shape[1] == BLOCK and features_b.shape[1] % 16 == 0
    return (local_four if suits else local_any)(features_a, features_b, *rest)


def solution(mesh):
    placed = (P("aa", "ba", None), P("ba", "aa", None), P(), P(), P())
    return jax.shard_map(
        local,
        mesh=mesh,
        in_specs=placed,
        out_specs=(P("aa", None, "ba", None), P("aa", "ba", None)),
        check_vma=False,
    )
```

```python
import functools
import math

import jax
import jax.numpy as jnp
from jax import lax
from jax.experimental import pallas as pl
from jax.experimental.pallas import tpu as pltpu
from jax.sharding import PartitionSpec as P

F32 = jnp.float32
BF16 = jnp.bfloat16
NT = (((1,), (1,)), ((), ()))
NN = (((1,), (0,)), ((), ()))
BLOCK = 8
HALF = 64
LANES = 128
LOG2E = math.log2(math.e)
FAR = 3e38
ORDERS = ((0, 1, 2, None), (None, 2, 1, 0))
GRANT = 20 * 1024 * 1024


class Sizes:
    def __init__(self, rows_a, width_a, rows_b, width_b, channels, hidden, grid_a, grid_b):
        self.rows_a, self.width_a = rows_a, width_a
        self.rows_b, self.width_b = rows_b, width_b
        self.channels, self.hidden = channels, hidden
        self.grid_a, self.grid_b = grid_a, grid_b
        self.blocks = width_a // BLOCK
        self.halo_a = rows_a + 4
        self.halo_b = rows_b + 4
        self.mid_a = rows_a + 2
        self.mid_b = rows_b + 2
        self.span = BLOCK + 2
        self.lanes_in = self.blocks * HALF
        self.lanes_mid = hidden * self.mid_a * BLOCK
        self.cells_a = rows_a * width_a
        self.cells_b = rows_b * width_b
        self.offset = math.log(grid_a * width_a * grid_b * width_b)
        self.scale = 1.0 / math.sqrt(channels)
        assert self.halo_a * self.span <= HALF and self.cells_a == HALF
        assert width_b == LANES and self.lanes_mid % LANES == 0
        assert self.blocks % 2 == 0


def iota(shape, dim):
    return lax.broadcasted_iota(jnp.int32, shape, dim)


def over_span(index, span):
    return (index * (2048 // span + 1)) >> 11


def dot(left, right, dims=NN):
    return lax.dot_general(left, right, dims, preferred_element_type=F32)


def vmem_specs(count):
    return [pl.BlockSpec(memory_space=pltpu.VMEM)] * count


def patch_lanes(sz, shape, dim):
    index = iota(shape, dim)
    block = index >> 6
    inner = index & (HALF - 1)
    row = over_span(inner, sz.span)
    col = block * BLOCK + inner - row * sz.span - 1
    inside = (inner < sz.halo_a * sz.span) & (col >= 0) & (col < sz.width_a)
    return row, col, inside


def taps_kernel(sz, w_in_ref, w_out_ref, bias_ref, t_in_ref, t_out_ref, bias_row_ref, rows_ref, wide_ref):
    lanes = sz.lanes_mid
    per = sz.mid_a * BLOCK
    head = iota((sz.hidden, lanes), 0)
    lane = iota((sz.hidden, lanes), 1)
    pick = (lane >= head * per) & (lane < head * per + per)
    pick16 = pick.astype(F32).astype(BF16)
    rows_ref[...] = dot(w_in_ref[...].astype(BF16), pick16)
    row_rank = lax.axis_index("aa")
    row = (iota((1, lanes), 1) // BLOCK) % sz.mid_a + row_rank * sz.rows_a - 1
    bias = jnp.sum(jnp.where(pick, bias_ref[...], 0.0), axis=0, keepdims=True)
    bias_row_ref[...] = jnp.where((row >= 0) & (row < sz.grid_a), bias, 0.0)
    inner = iota((HALF, lanes), 0)
    row_in = over_span(inner, sz.span)
    col_in = inner - row_in * sz.span
    lane = iota((HALF, lanes), 1)
    row_out = (lane // BLOCK) % sz.mid_a
    col_out = lane % BLOCK
    step_row = row_in - row_out
    step_col = col_in - col_out
    from_row = row_in + row_rank * sz.rows_a - 2
    to_row = row_out + row_rank * sz.rows_a - 1
    usable = (inner < sz.halo_a * sz.span) & (from_row >= 0) & (from_row < sz.grid_a)
    usable = usable & (to_row >= 0) & (to_row < sz.grid_a)
    zeros = jnp.zeros((HALF, lanes), F32)
    for three in range(3):
        for four in range(3):
            total = zeros
            for one in range(3):
                for two in range(3):
                    tap = ((one * 3 + two) * 3 + three) * 3 + four
                    match = usable & (step_row == one) & (step_col == two)
                    total = jnp.where(match, rows_ref[tap : tap + 1, :], total)
            for side in range(2):
                start = ((side * 3 + three) * 4 + ORDERS[side].index(four)) * HALF
                t_in_ref[start : start + HALF, :] = total.astype(BF16)
        for side in range(2):
            start = ((side * 3 + three) * 4 + ORDERS[side].index(None)) * HALF
            t_in_ref[start : start + HALF, :] = zeros.astype(BF16)

    out_lanes = 4 * HALF
    unit = sz.rows_a * BLOCK
    group = 9 * sz.hidden
    for row in range(sz.mid_a):
        pair = iota((16, out_lanes), 0)
        lane = iota((16, out_lanes), 1)
        one = pair // 3
        four = pair - one * 3
        row_out = (lane % unit) // BLOCK
        hit = (pair < 9) & ((lane >> 6) == four) & (row - row_out == one)
        wide_ref[row * group : (row + 1) * group, :] = dot(
            w_out_ref[...].astype(BF16), hit.astype(F32).astype(BF16)
        )
    lane = iota((BLOCK, out_lanes), 1)
    col_out = ((lane & (HALF - 1)) // unit) * BLOCK + lane % BLOCK
    for block in range(sz.blocks):
        step = iota((BLOCK, out_lanes), 0) + block * BLOCK - col_out + 1
        for three in range(3):
            for head in range(sz.hidden):
                for row in range(0, sz.mid_a, 2):
                    parts = []
                    for sub in (row, row + 1):
                        total = jnp.zeros((BLOCK, out_lanes), F32)
                        for two in range(3):
                            at = sub * group + (two * 3 + three) * sz.hidden + head
                            total = jnp.where(step == two, wide_ref[at : at + 1, :], total)
                        parts.append(total)
                    start = three * sz.blocks * lanes + block * lanes + head * per + row * BLOCK
                    t_out_ref[start : start + 2 * BLOCK, :] = jnp.concatenate(parts, 0).astype(BF16)


def build_taps(sz, conv_in, bias_in, conv_out):
    hidden = conv_in.shape[0]
    w_in = jnp.transpose(conv_in, (1, 2, 3, 4, 0)).reshape(81, hidden)
    w_out = jnp.transpose(conv_out, (2, 3, 0, 1, 4)).reshape(9 * hidden, 9)
    w_out = jnp.pad(w_out, ((0, 0), (0, 7)))
    rows_in = 2 * 3 * 4 * HALF
    rows_out = 3 * sz.blocks * sz.lanes_mid
    return pl.pallas_call(
        functools.partial(taps_kernel, sz),
        out_shape=(
            jax.ShapeDtypeStruct((rows_in, sz.lanes_mid), BF16),
            jax.ShapeDtypeStruct((rows_out, 4 * HALF), BF16),
            jax.ShapeDtypeStruct((1, sz.lanes_mid), F32),
        ),
        in_specs=vmem_specs(3),
        out_specs=tuple(vmem_specs(3)),
        scratch_shapes=[
            pltpu.VMEM((81, sz.lanes_mid), F32),
            pltpu.VMEM((sz.mid_a * 9 * hidden, 4 * HALF), F32),
        ],
        compiler_params=pltpu.CompilerParams(vmem_limit_bytes=GRANT),
        name="taps",
    )(w_in, w_out, bias_in.reshape(hidden, 1))


def spread_kernel(a_ref, b_ref, out_ref):
    cells = a_ref.shape[0]
    for at in range(out_ref.shape[0]):
        out_ref[at, 0:cells, :] = a_ref[...]
        out_ref[at, cells:, :] = b_ref[...]


def scores_body(sz, norm_rows, patch_rows, tile_b, u_ref, part_ref, near_ref, all_ref):
    source = patch_rows.shape[0]
    row, col, inside = patch_lanes(sz, (sz.lanes_in, source), 0)
    at = iota((sz.lanes_in, source), 1)
    wanted = (col >> 3) * (sz.halo_a * BLOCK) + row * BLOCK + (col & (BLOCK - 1))
    pick = (inside & (at == wanted)).astype(F32).astype(BF16)
    patches = dot(pick, patch_rows[...]).astype(BF16)
    near_ref[...] = dot(tile_b[...], patches, NT)
    all_ref[...] = dot(tile_b[...], norm_rows[...], NT)
    steep = sz.scale * LOG2E
    for index in range(sz.halo_b):
        place = slice(index * LANES, (index + 1) * LANES)
        best = jnp.max(all_ref[place, :], axis=1, keepdims=True)
        mass = jnp.sum(jnp.exp2((all_ref[place, :] - best) * steep), axis=1, keepdims=True)
        shift = sz.offset - (best * sz.scale + jnp.log(mass))
        u_ref[place, :] = near_ref[place, :] * (2.0 * sz.scale) + shift
    own = slice(2 * LANES, (2 + sz.rows_b) * LANES)
    best = jnp.max(near_ref[own, :], axis=0, keepdims=True)
    mass = jnp.sum(jnp.exp2((near_ref[own, :] - best) * steep), axis=0, keepdims=True)
    part_ref[...] = jnp.concatenate(
        [best * sz.scale, mass, jnp.zeros((6, sz.lanes_in), F32)], axis=0
    )


def scores_kernel_direct(sz, norm_rows, patch_rows, tile_b, u_ref, part_ref, near_ref, all_ref):
    scores_body(sz, norm_rows, patch_rows, tile_b, u_ref, part_ref, near_ref, all_ref)


def scores_kernel_pieces(
    sz, count, own_piece, core_piece, cross_piece, diag_piece,
    u_ref, part_ref, own_a_ref, own_b_ref,
    norm_rows, patch_rows, tile_b, near_ref, all_ref,
):
    row_rank, col_rank = lax.axis_index("aa"), lax.axis_index("ba")
    cells = sz.rows_a * BLOCK
    cols = sz.width_b // count
    pieces = ((own_piece, 0), (core_piece, 1), (diag_piece, 2), (cross_piece, 3))
    for order, (piece, flip) in enumerate(pieces):
        norm_rows[order * count * cells : (order + 1) * count * cells, :] = piece[
            :, 0:cells, :
        ].reshape(count * cells, sz.channels)
        block = col_rank ^ flip
        for step in range(3):
            where_from = jnp.clip(row_rank - 1 + step, 0, count - 1)
            start = pl.multiple_of(block * (3 * cells) + step * cells, cells)
            patch_rows[pl.ds(start, cells), :] = piece[where_from, 0:cells, :]
        start = pl.multiple_of(block * cells, cells)
        own_a_ref[pl.ds(start, cells), :] = piece[row_rank, 0:cells, :]
    width = sz.width_b
    for row in range(sz.rows_b):
        rows = own_piece[:, cells + row * cols : cells + (row + 1) * cols, :].reshape(width, sz.channels)
        tile_b[(2 + row) * width : (3 + row) * width, :] = rows
        own_b_ref[row * width : (row + 1) * width, :] = rows
    odd = col_rank & 1
    far = (2 + sz.rows_b) * width
    for piece, base in ((core_piece, (1 - odd) * far), (cross_piece, odd * far)):
        for row in range(2):
            rows = piece[:, cells + row * cols : cells + (row + 1) * cols, :].reshape(width, sz.channels)
            tile_b[pl.ds(pl.multiple_of(base + row * width, width), width), :] = rows
    scores_body(sz, norm_rows, patch_rows, tile_b, u_ref, part_ref, near_ref, all_ref)


def softplus(values):
    return jnp.maximum(values, 0.0) + jnp.log(1.0 + jnp.exp(-jnp.abs(values)))


def refine_kernel(sz, parts, u_ref, *refs):
    part_refs = refs[:parts]
    t_in, t_out, bias_row, own_a, own_b, refined_ref, sums_ref, pad_ref, x_ref, mid_ref = refs[parts:]
    col_rank = lax.axis_index("ba")
    last = sz.grid_b // sz.rows_b - 1
    tops, masses = [], []
    for ref in part_refs:
        for at in range(ref.shape[0] // 8):
            tops.append(ref[at * 8 : at * 8 + 1, :])
            masses.append(ref[at * 8 + 1 : at * 8 + 2, :])
    top = functools.reduce(jnp.maximum, tops)
    mass = sum(m * jnp.exp(t - top) for t, m in zip(tops, masses))
    norm_b = top + jnp.log(mass)

    row, _, inside = patch_lanes(sz, (1, sz.lanes_in), 1)
    norm_b = jnp.where(inside, norm_b, FAR)
    low = iota((LANES, LANES), 1) < HALF
    line = iota((LANES, LANES), 0)
    rows_mid = sz.mid_b * LANES
    depth = 3 * 4 * HALF
    bias = bias_row[...]
    for pair in range(sz.blocks // 2):
        lanes = slice(pair * LANES, (pair + 1) * LANES)
        for index in range(sz.halo_b):
            norm = norm_b[:, lanes]
            if index < 2:
                norm = jnp.where(col_rank == 0, FAR, norm)
            if index >= sz.halo_b - 2:
                norm = jnp.where(col_rank == last, FAR, norm)
            place = slice(index * LANES, (index + 1) * LANES)
            matched = softplus(u_ref[place, lanes] - norm)
            pad_ref[pair, index, 0:8, :] = jnp.zeros((8, LANES), F32)
            pad_ref[pair, index, 8 + LANES :, :] = jnp.zeros((8, LANES), F32)
            pad_ref[pair, index, 8 : 8 + LANES, :] = matched
            turned = pltpu.roll(matched, HALF, 1)
            down = pad_ref[pair, index, 7 : 7 + LANES, :]
            x_ref[pair, place, 0:LANES] = jnp.where(low, down, turned).astype(BF16)
            x_ref[pair, place, LANES : 2 * LANES] = pad_ref[pair, index, 9 : 9 + LANES, :].astype(BF16)
            x_ref[pair, place, 2 * LANES :] = jnp.where(low, turned, down).astype(BF16)
        for side in range(2):
            lanes = slice(side * LANES, (side + 2) * LANES)
            stacked = jnp.concatenate(
                [x_ref[pair, three * LANES : three * LANES + rows_mid, lanes] for three in range(3)], axis=1
            )
            total = dot(stacked, t_in[side * depth : (side + 1) * depth, :]) + bias
            hidden = jnp.maximum(total, 0.0).astype(BF16)
            start = (pair * 2 + side) * sz.lanes_mid
            lanes = slice(start, start + sz.lanes_mid)
            head, tail = hidden[0:LANES], hidden[rows_mid - LANES :]
            mid_ref[0:LANES, lanes] = jnp.where(col_rank == 0, jnp.zeros_like(head), head)
            mid_ref[LANES : rows_mid - LANES, lanes] = hidden[LANES : rows_mid - LANES]
            mid_ref[rows_mid - LANES :, lanes] = jnp.where(col_rank == last, jnp.zeros_like(tail), tail)
    stacked = jnp.concatenate(
        [mid_ref[three * LANES : three * LANES + sz.cells_b, :] for three in range(3)], axis=1
    )
    spread = dot(stacked, t_out[...])
    tops, masses = [], []
    for row in range(sz.rows_b):
        left = spread[row * LANES : (row + 1) * LANES, 0:LANES]
        right = spread[row * LANES : (row + 1) * LANES, LANES : 2 * LANES]
        filtered = (
            jnp.where(line > 0, pltpu.roll(left, 1, 0), 0.0)
            + pltpu.roll(left, HALF, 1)
            + jnp.where(line < LANES - 1, pltpu.roll(right, LANES - 1, 0), 0.0)
        )
        filtered = jnp.maximum(filtered, 0.0).T[0:HALF, :]
        scores = dot(own_a[...], own_b[row * LANES : (row + 1) * LANES, :], NT) * sz.scale
        refined = scores + filtered
        refined_ref[:, row * LANES : (row + 1) * LANES] = refined
        tops.append(jnp.max(refined, axis=0, keepdims=True))
        masses.append(jnp.sum(jnp.exp(refined - tops[-1]), axis=0, keepdims=True))
    sums = jnp.concatenate(tops + masses, axis=0)
    for at in range(sums_ref.shape[0]):
        sums_ref[at] = sums


def share_kernel(sz, split, refined_ref, own_b, *refs):
    best_b = jnp.max(refined_ref[...], axis=1, keepdims=True)
    weights = jnp.exp(refined_ref[...] - best_b)
    total_b = jnp.sum(weights, axis=1, keepdims=True)
    high = weights.astype(BF16)
    rest = (weights - high.astype(F32)).astype(BF16)
    share = dot(high, own_b[...]) + dot(rest, own_b[...])
    lane = iota((HALF, LANES), 1)
    stats = jnp.where(lane < HALF, best_b, total_b)
    if not split:
        refs[0][...] = share
        refs[1][...] = stats
        return
    share_ref = refs[4]
    share_ref[...] = share
    cells = sz.rows_a * BLOCK
    for flip in range(4):
        start = pl.multiple_of((lax.axis_index("ba") ^ flip) * cells, cells)
        refs[flip][0:cells, :] = share_ref[pl.ds(start, cells), :]
        refs[flip][cells:, 0:LANES] = stats[0 : HALF // 2, :]
        refs[flip][cells:, LANES:] = stats[HALF // 2 :, :]


def finish_kernel(sz, count, refined_ref, sums_ref, own, core, diag, cross, out_ref, warped_ref, stat_ref):
    col_rank = lax.axis_index("ba")
    cells = sz.rows_a * BLOCK
    lane = iota((HALF, LANES), 1)
    tops, masses = [], []
    for at, ref in enumerate((own, core, diag, cross)):
        stats = jnp.concatenate([ref[cells:, 0:LANES], ref[cells:, LANES:]], axis=0)
        turned = pltpu.roll(stats, HALF, 1)
        tops.append(jnp.where(lane < HALF, stats, turned))
        masses.append(jnp.where(lane < HALF, turned, stats))
        stat_ref[at] = tops[-1]
    top = functools.reduce(jnp.maximum, tops)
    norm_b = top + jnp.log(sum(m * jnp.exp(t - top) for t, m in zip(tops, masses)))
    stat_ref[4] = norm_b
    mine = pl.ds(pl.multiple_of(col_rank * cells, cells), cells)
    norm_mine = stat_ref[4, mine, :]
    warped = 0.0
    for at, ref in enumerate((own, core, diag, cross)):
        factor = jnp.exp(stat_ref[at, mine, :] - norm_mine)
        warped = warped + ref[0:cells, :] * jnp.concatenate(
            [factor] * (sz.channels // LANES), axis=1
        )
    warped_ref[...] = warped.reshape(sz.rows_a, BLOCK, sz.channels)
    tops = [sums_ref[at * 8 : at * 8 + sz.rows_b, :] for at in range(count)]
    masses = [sums_ref[at * 8 + sz.rows_b : at * 8 + 2 * sz.rows_b, :] for at in range(count)]
    top = functools.reduce(jnp.maximum, tops)
    norm_a = top + jnp.log(sum(m * jnp.exp(t - top) for t, m in zip(tops, masses)))
    for row in range(sz.rows_b):
        values = (
            2.0 * refined_ref[:, row * LANES : (row + 1) * LANES]
            - norm_a[row : row + 1, :]
            - norm_b
            + sz.offset
        )
        for block in range(sz.blocks):
            for high in range(sz.rows_a):
                start = block * cells + high * BLOCK
                out_ref[high, block * BLOCK : (block + 1) * BLOCK, row, :] = values[start : start + BLOCK, :]


def call(kernel, name, outs, scratch, *args):
    return pl.pallas_call(
        kernel,
        out_shape=outs,
        in_specs=vmem_specs(len(args)),
        out_specs=tuple(vmem_specs(len(outs))),
        scratch_shapes=scratch,
        compiler_params=pltpu.CompilerParams(vmem_limit_bytes=GRANT),
        name=name,
    )(*args)


def refine_call(sz, parts, copies, *args):
    shape = jax.ShapeDtypeStruct
    outs = (shape((HALF, sz.cells_b), F32), shape((copies, 8, LANES), F32))
    scratch = [
        pltpu.VMEM((sz.blocks // 2, sz.halo_b, LANES + 16, LANES), F32),
        pltpu.VMEM((sz.blocks // 2, sz.halo_b * LANES, 3 * LANES), BF16),
        pltpu.VMEM((sz.mid_b * LANES, sz.blocks * sz.lanes_mid), BF16),
    ]
    return call(functools.partial(refine_kernel, sz, parts), "refine", outs, scratch, *args)


def share_call(sz, split, *args):
    shape = jax.ShapeDtypeStruct
    if split:
        outs = (shape((sz.rows_a * BLOCK + HALF // 2, 2 * LANES), F32),) * 4
        scratch = [pltpu.VMEM((HALF, sz.channels), F32)]
    else:
        outs = (shape((HALF, sz.channels), F32), shape((HALF, LANES), F32))
        scratch = []
    return call(functools.partial(share_kernel, sz, split), "share", outs, scratch, *args)


def swap(value, flip, count):
    return lax.ppermute(value, "ba", [(at, at ^ flip) for at in range(count)])


def sizes_of(features_a, features_b, conv_in):
    rows_a, cols_a, channels = features_a.shape
    rows_b, cols_b, _ = features_b.shape
    count_a, count_b = lax.axis_size("aa"), lax.axis_size("ba")
    return Sizes(
        rows_a, cols_a * count_b, rows_b, cols_b * count_a, channels, conv_in.shape[0],
        rows_a * count_a, rows_b * count_b,
    )


def local_four(features_a, features_b, conv_in, bias_in, conv_out):
    sz = sizes_of(features_a, features_b, conv_in)
    count = lax.axis_size("aa")
    shape = jax.ShapeDtypeStruct
    col_rank = lax.axis_index("ba")
    cells = sz.rows_a * BLOCK
    cols = features_b.shape[1]
    fine_a = features_a.reshape(cells, sz.channels)
    fine_b = features_b.reshape(-1, sz.channels)
    (spread,) = call(
        spread_kernel,
        "spread",
        (shape((count, cells + fine_b.shape[0], sz.channels), BF16),),
        [],
        fine_a, fine_b,
    )
    own = lax.all_to_all(spread, "aa", 0, 0, tiled=True)
    rows_here = own[:, 0:cells]
    first = own[:, cells : cells + 2 * cols]
    final = own[:, cells + (sz.rows_b - 2) * cols :]
    odd = (col_rank & 1) == 1
    core = swap(jnp.concatenate([rows_here, jnp.where(odd, first, final)], axis=1), 1, 4)
    cross = swap(jnp.concatenate([rows_here, jnp.where(odd, final, first)], axis=1), 3, 4)
    diag = swap(rows_here, 2, 4)
    t_in, t_out, bias_row = build_taps(sz, conv_in, bias_in, conv_out)
    u, part, own_a, own_b = call(
        functools.partial(scores_kernel_pieces, sz, count),
        "scores",
        (
            shape((sz.halo_b * LANES, sz.lanes_in), F32),
            shape((8, sz.lanes_in), F32),
            shape((HALF, sz.channels), BF16),
            shape((sz.cells_b, sz.channels), BF16),
        ),
        [
            pltpu.VMEM((sz.grid_a * sz.width_a, sz.channels), BF16),
            pltpu.VMEM((sz.halo_a * sz.width_a, sz.channels), BF16),
            pltpu.VMEM((sz.halo_b * LANES, sz.channels), BF16),
            pltpu.VMEM((sz.halo_b * LANES, sz.lanes_in), F32),
            pltpu.VMEM((sz.halo_b * LANES, sz.grid_a * sz.width_a), F32),
        ],
        own, core, cross, diag,
    )
    others = [swap(part, flip, 4) for flip in (1, 3, 2)]
    refined, sums = refine_call(
        sz, 4, count, u, part, *others, t_in, t_out, bias_row, own_a, own_b
    )
    sums = lax.all_to_all(sums, "aa", 0, 0, tiled=True).reshape(count * 8, LANES)
    bundles = share_call(sz, True, refined, own_b)
    moved = [swap(bundles[flip], flip, 4) for flip in (1, 3, 2)]
    return call(
        functools.partial(finish_kernel, sz, count),
        "finish",
        (
            shape((sz.rows_a, sz.width_a, sz.rows_b, LANES), F32),
            shape((sz.rows_a, BLOCK, sz.channels), F32),
        ),
        [pltpu.VMEM((5, HALF, LANES), F32)],
        refined, sums, bundles[0], moved[0], moved[2], moved[1],
    )


def local_any(features_a, features_b, conv_in, bias_in, conv_out):
    sz = sizes_of(features_a, features_b, conv_in)
    count_b = lax.axis_size("ba")
    shape = jax.ShapeDtypeStruct
    row_rank = lax.axis_index("aa")
    channels = sz.channels
    rows_a = lax.all_gather(features_a, "ba", axis=1, tiled=True)
    all_a = lax.all_gather(rows_a, "aa", axis=0, tiled=True)
    around = lax.dynamic_slice_in_dim(
        jnp.pad(all_a, ((2, 2), (0, 0), (0, 0))), row_rank * sz.rows_a, sz.halo_a, axis=0
    )

    def blocked(rows):
        split = rows.reshape(rows.shape[0], sz.blocks, BLOCK, channels)
        return jnp.transpose(split, (1, 0, 2, 3)).reshape(-1, channels)

    rows_b = lax.all_gather(features_b, "aa", axis=1, tiled=True)
    ends = count_b - 1
    before = lax.ppermute(rows_b[-2:], "ba", [(at, at + 1) for at in range(ends)])
    after = lax.ppermute(rows_b[:2], "ba", [(at + 1, at) for at in range(ends)])
    tile_b = jnp.concatenate([before, rows_b, after], axis=0).reshape(-1, channels)
    t_in, t_out, bias_row = build_taps(sz, conv_in, bias_in, conv_out)
    u, part = call(
        functools.partial(scores_kernel_direct, sz),
        "scores",
        (shape((sz.halo_b * LANES, sz.lanes_in), F32), shape((8, sz.lanes_in), F32)),
        [
            pltpu.VMEM((sz.halo_b * LANES, sz.lanes_in), F32),
            pltpu.VMEM((sz.halo_b * LANES, sz.grid_a * sz.width_a), F32),
        ],
        all_a.reshape(-1, channels), blocked(around), tile_b,
    )
    parts = lax.all_gather(part, "ba", axis=0, tiled=True)
    whole_b = rows_b.reshape(-1, channels)
    refined, sums_a = refine_call(
        sz, 1, 1, u, parts, t_in, t_out, bias_row, blocked(rows_a), whole_b
    )
    sums_a = sums_a[0]
    share, stats = share_call(sz, False, refined, whole_b)
    top, mass = stats[:, 0], stats[:, HALF]
    best = lax.pmax(top, "ba")
    norm_b = best + jnp.log(lax.psum(mass * jnp.exp(top - best), "ba"))

    def unblocked(rows):
        split = rows.reshape((sz.blocks, sz.rows_a, BLOCK) + rows.shape[1:])
        return jnp.swapaxes(split, 0, 1).reshape((sz.rows_a, sz.width_a) + rows.shape[1:])

    share = unblocked(share * jnp.exp(top - norm_b)[:, None])
    warped = lax.psum_scatter(share, "ba", scatter_dimension=1, tiled=True)
    top, mass = sums_a[: sz.rows_b], sums_a[sz.rows_b : 2 * sz.rows_b]
    best = lax.pmax(top, "aa")
    norm_a = best + jnp.log(lax.psum(mass * jnp.exp(top - best), "aa"))
    refined = refined.reshape(HALF, sz.rows_b, LANES)
    mutual = 2.0 * refined - norm_a - norm_b[:, None, None] + sz.offset
    return unblocked(mutual), warped


def local(features_a, features_b, *rest):
    suits = lax.axis_size("ba") == 4 and features_a.shape[1] == BLOCK and features_b.shape[1] % 16 == 0
    return (local_four if suits else local_any)(features_a, features_b, *rest)


def solution(mesh):
    placed = (P("aa", "ba", None), P("ba", "aa", None), P(), P(), P())
    return jax.shard_map(
        local,
        mesh=mesh,
        in_specs=placed,
        out_specs=(P("aa", None, "ba", None), P("aa", "ba", None)),
        check_vma=False,
    )
```
